256 devices in a mesh: grp: 8 (over x, core), seq: 32 (over y, z).
Axes of the slice: x: 4, y: 4, z: 8, core: 2. Of those that a mesh axis runs over, the one named last changes fastest.
Arguments:
- queries: bfloat16 [1, 32768, 2048], P(None, ('grp', 'seq')), may hold values from -6 to 6
- key_vectors: bfloat16 [1, 32768, 2048], P(None, ('grp', 'seq')), may hold values from -6 to 6
- values: bfloat16 [1, 32768, 2048], P(None, ('grp', 'seq')), may hold values from -6 to 6
- log_decay: bfloat16 [1, 32768, 2048], P(None, ('grp', 'seq')), may hold values from -0.8 to 0, as said below
- write_rate: float32 [1, 16, 32768], P(None, None, ('grp', 'seq')), may hold values from 0 to 1, as said below
- out_gate: bfloat16 [1, 32768, 2048], P(None, ('grp', 'seq')), may hold values from -6 to 6
Outputs:
- layer_output: bfloat16 [1, 32768, 2048], P(None, ('grp', 'seq'))
The draws below stay inside these ranges and needn't reach their ends.
Inputs may be any that keep to these rules, and one draw needn't show every extreme that they name: log_decay is negative. write_rate is positive.
All inputs are finite; a program needn't handle non-finite values.
Results may differ from the reference program's by a relative error of at most 0.001.
Values sent between devices are 32-bit elements; how exact they have to be, the bound alone decides.
No kernel may reach another device: no remote copies, remote signals or barrier semaphores. Data moves between devices by JAX's collectives and lax.ppermute only.
A program may use at most 128 MiB of HBM per device.

```python
import math
import jax
import jax.numpy as jnp
from jax import lax

LOCAL_HEADS = 16
DK = 128
BLOCK = 64
SEQUENCE_COUNT = 1
TOK_DEV = 128
SEQUENCE_LENGTH = 32768


def slow_heads(key):
    kind_key = jax.random.fold_in(key, 11)
    slow_share = 0.5
    return jax.random.uniform(kind_key, (SEQUENCE_COUNT, LOCAL_HEADS)) < slow_share


def draw_log_decay(key, part):
    picked_heads = slow_heads(key)
    random_subkeys = jax.random.split(jax.random.fold_in(key, 23), 5)
    channel_key = jax.random.fold_in(key, 29)
    gentle_channels = jax.random.uniform(channel_key, (SEQUENCE_COUNT, 1, LOCAL_HEADS, DK)) < 0.25
    segments = SEQUENCE_LENGTH // TOK_DEV
    segment = jnp.exp(jax.random.uniform(random_subkeys[0], (SEQUENCE_COUNT, segments, 1, 1), minval=-math.log(2.0), maxval=math.log(2.0)))
    segment = jnp.repeat(segment, TOK_DEV, axis=1)
    gentle = jnp.exp(jax.random.uniform(random_subkeys[1], (SEQUENCE_COUNT, SEQUENCE_LENGTH, LOCAL_HEADS, DK), minval=math.log(0.05), maxval=math.log(0.5))) / SEQUENCE_LENGTH
    strong = jnp.exp(jax.random.uniform(random_subkeys[2], (SEQUENCE_COUNT, SEQUENCE_LENGTH, LOCAL_HEADS, DK), minval=math.log(1.0 / 50.0), maxval=math.log(1.0 / 30.0)))
    use_gentle = jnp.logical_or(picked_heads[:, None, :, None], gentle_channels)
    rate_values = jnp.where(use_gentle, gentle, strong) * segment
    token_positions = jax.random.randint(random_subkeys[3], (SEQUENCE_COUNT, 3), 0, SEQUENCE_LENGTH)
    spike_locations = jnp.arange(SEQUENCE_LENGTH, dtype=jnp.int32)
    spike_selected = jnp.any(spike_locations[None, :, None] == token_positions[:, None, :], axis=-1)
    spike_lowering = jax.random.uniform(random_subkeys[4], (SEQUENCE_COUNT, SEQUENCE_LENGTH, LOCAL_HEADS, 1), minval=math.log(0.5), maxval=math.log(0.8))
    applied_rates = jnp.logical_and(spike_selected[:, :, None, None], picked_heads[:, None, :, None])
    final_output = -rate_values + jnp.where(applied_rates, spike_lowering, 0.0)
    return final_output.reshape(SEQUENCE_COUNT, SEQUENCE_LENGTH, LOCAL_HEADS * DK).astype(jnp.bfloat16)


def draw_write_rate(key, part):
    picked_heads = slow_heads(key)
    random_subkeys = jax.random.split(jax.random.fold_in(key, 31), 2)
    gentle = jax.random.uniform(random_subkeys[0], (SEQUENCE_COUNT, LOCAL_HEADS, SEQUENCE_LENGTH), minval=0.3, maxval=1.0) * DK / SEQUENCE_LENGTH
    strong = jax.random.uniform(random_subkeys[1], (SEQUENCE_COUNT, LOCAL_HEADS, SEQUENCE_LENGTH), minval=0.1, maxval=1.0)
    return jnp.where(picked_heads[:, :, None], gentle, strong).astype(jnp.float32)


def shard_levels(key, shape, cuts, least, top_value):
    factor_of, own = 1.0, jax.random.fold_in(key, 6)
    for dim, shards_of in cuts:
        draws = jnp.exp(jax.random.uniform(jax.random.fold_in(own, dim), (shards_of,), jnp.float32, least / len(cuts), top_value / len(cuts)))
        factor_of = factor_of * jnp.repeat(draws, shape[dim] // shards_of).reshape([-1 if axis == dim else 1 for axis in range(len(shape))])
    return factor_of


def bell_draw(rng, shape, spread, limit, cuts=(), held_as=jnp.bfloat16):
    values = spread * jax.random.normal(rng, shape, jnp.float32)
    if cuts:
        values = values * shard_levels(rng, shape, cuts, -0.22, 0.18)
    return jnp.clip(values, -limit, limit).astype(held_as)


def setup_inputs(seed: int = 0) -> dict:
    key_of = jax.random.split(jax.random.key(seed), 7)
    queries = bell_draw(key_of[0], (SEQUENCE_COUNT, SEQUENCE_LENGTH, LOCAL_HEADS * DK), 1.0, 6.0, ((1, 256),))
    key_vectors = bell_draw(key_of[1], (SEQUENCE_COUNT, SEQUENCE_LENGTH, LOCAL_HEADS * DK), 1.0, 6.0, ((1, 256),))
    values = bell_draw(key_of[2], (SEQUENCE_COUNT, SEQUENCE_LENGTH, LOCAL_HEADS * DK), 1.0, 6.0, ((1, 256),))
    log_decay = draw_log_decay(jax.random.fold_in(key_of[6], 71), 0)
    write_rate = draw_write_rate(jax.random.fold_in(key_of[6], 71), 0)
    out_gate = bell_draw(key_of[5], (SEQUENCE_COUNT, SEQUENCE_LENGTH, LOCAL_HEADS * DK), 1.5, 6.0, ((1, 256),))
    return dict(queries=queries, key_vectors=key_vectors, values=values, log_decay=log_decay, write_rate=write_rate, out_gate=out_gate)


precise_mode = lax.Precision.HIGHEST

def matmul(left, right):
    return jnp.einsum('...ij,...jk->...ik', left, right, precision=precise_mode)

def inner_rows(left, right):
    return jnp.einsum('...ci,...cj->...ij', left, right, precision=precise_mode)

def outer_rows(left, right):
    return jnp.einsum('...tc,...sc->...ts', left, right, precision=precise_mode)

def unit_lower_inverse(lower_part):
    extent = lower_part.shape[-1]
    identity = jnp.eye(extent, dtype=lower_part.dtype)
    powered = lower_part
    inverse = identity - lower_part
    for squaring in range(extent.bit_length() - 2):
        powered = matmul(powered, powered)
        inverse = matmul(inverse, identity + powered)
    return inverse

def block_terms(query_f, key_unit, decay_log, rate_block):
    extent = query_f.shape[-2]
    cumulative = jnp.cumsum(decay_log, axis=-2)
    growing = jnp.exp(cumulative)
    shrinking = jnp.exp(-cumulative)
    to_end = jnp.exp(cumulative[..., -1:, :] - cumulative)
    key_grow = key_unit * growing
    key_shrink = key_unit * shrinking
    query_grow = query_f * growing
    key_end = key_unit * to_end * rate_block[..., None]
    row_ids = lax.broadcasted_iota(jnp.int32, (extent, extent), 0)
    col_ids = lax.broadcasted_iota(jnp.int32, (extent, extent), 1)
    affinity = outer_rows(key_grow, key_shrink) * rate_block[..., None, :]
    lower_part = jnp.where(row_ids > col_ids, affinity, 0.0)
    attend = jnp.where(row_ids >= col_ids, outer_rows(query_grow, key_shrink) * rate_block[..., None, :], 0.0)
    inverse = unit_lower_inverse(lower_part)
    decay_end = jnp.exp(cumulative[..., -1, :])
    return (query_grow, key_grow, key_end, attend, inverse, decay_end)

def reference(queries, key_vectors, values, log_decay, write_rate, out_gate):
    seq_count, seq_len, features = queries.shape
    blocks = seq_len // BLOCK

    def to_blocks(tensor):
        shaped = tensor.reshape(seq_count, blocks, BLOCK, LOCAL_HEADS, DK)
        return jnp.transpose(shaped, (1, 0, 3, 2, 4))
    rate_blocks = jnp.transpose(write_rate.reshape(seq_count, LOCAL_HEADS, blocks, BLOCK), (2, 0, 1, 3))

    def advance(memory, inputs):
        query_in, key_in, value_in, decay_in, rate_in, gate_in = inputs
        query_f = query_in.astype(jnp.float32)
        key_f = key_in.astype(jnp.float32)
        key_unit = key_f / jnp.sqrt(lax.optimization_barrier(jnp.sum(key_f * key_f, axis=-1, keepdims=True)) + 1e-06)
        query_grow, key_grow, key_end, attend, inverse, decay_end = block_terms(query_f, key_unit, decay_in.astype(jnp.float32), rate_in)
        fresh_vals = matmul(inverse, value_in.astype(jnp.float32) - matmul(key_grow, memory))
        raw_out = matmul(query_grow, memory) + matmul(attend, fresh_vals)
        memory = decay_end[..., :, None] * memory + inner_rows(key_end, fresh_vals)
        scaled = raw_out / jnp.sqrt(lax.optimization_barrier(jnp.mean(raw_out * raw_out, axis=-1, keepdims=True)) + 1e-05)
        final_output = (scaled * jax.nn.sigmoid(gate_in.astype(jnp.float32))).astype(jnp.bfloat16)
        return (memory, final_output)
    initial = jnp.zeros((seq_count, LOCAL_HEADS, DK, DK), jnp.float32)
    _, results = lax.scan(advance, initial, (to_blocks(queries), to_blocks(key_vectors), to_blocks(values), to_blocks(log_decay), rate_blocks, to_blocks(out_gate)))
    return jnp.transpose(results, (1, 0, 3, 2, 4)).reshape(seq_count, seq_len, features)
```

```python
import functools

import jax
import jax.numpy as jnp
from jax import lax
from jax.experimental import pallas as pl
from jax.experimental.pallas import tpu as pltpu
from jax.sharding import PartitionSpec as P

DK = 128
TOK = 128
CHUNK = 8
F32 = jnp.float32
BF16 = jnp.bfloat16


def split(x):
    hi = x.astype(BF16)
    return hi, (x - hi.astype(F32)).astype(BF16)


def raw_dot(a, b, nt=False):
    dims = (((1,), (1 if nt else 0,)), ((), ()))
    return lax.dot_general(a, b, dims, preferred_element_type=F32)


def dot_split(a, b, nt=False):
    (ah, al), (bh, bl) = a, b
    return raw_dot(ah, bh, nt) + (raw_dot(ah, bl, nt) + raw_dot(al, bh, nt))


def dot3(a, b, nt=False):
    return dot_split(split(a), split(b), nt)


def ids(extent):
    rows = lax.broadcasted_iota(jnp.int32, (extent, extent), 0)
    cols = lax.broadcasted_iota(jnp.int32, (extent, extent), 1)
    return rows, cols


def unit_keys(key):
    key = key.astype(F32)
    return key * lax.rsqrt(jnp.sum(key * key, axis=-1, keepdims=True) + 1e-06)


def decay_sums(decay, rows, cols):
    tri = jnp.where(rows >= cols, 1.0, 0.0).astype(BF16)
    return raw_dot(tri, decay)


def maps_kernel(heads, k_ref, v_ref, g_ref, rate_ref, ma_ref, wu_ref):
    rows, cols = ids(TOK)
    eye = jnp.where(rows == cols, 1.0, 0.0)
    base = pl.program_id(0) * heads
    each = range(heads)
    lane = [slice(h * DK, (h + 1) * DK) for h in each]
    rate = [rate_ref[0, pl.ds(base + h, 1), :] for h in each]
    sums = [decay_sums(g_ref[0, :, lane[h]], rows, cols) for h in each]
    unit = [unit_keys(k_ref[0, :, lane[h]]) for h in each]
    mid = [s[TOK // 2 - 1 : TOK // 2, :] for s in sums]
    end = [s[TOK - 1 :, :] for s in sums]
    grow = [unit[h] * jnp.exp(sums[h] - mid[h]) for h in each]
    shrink = [unit[h] * jnp.exp(mid[h] - sums[h]) for h in each]
    affinity = [dot3(grow[h], shrink[h], nt=True) * rate[h] for h in each]
    lower = [jnp.where(rows > cols, a, 0.0) for a in affinity]
    apart = rows ^ cols
    inverse = [eye - jnp.where(apart < 2, lo, 0.0) for lo in lower]
    extent = 2
    while extent < TOK:
        joint = (apart >= extent) & (apart < 2 * extent)
        parts = [split(inv) for inv in inverse]
        inner = [
            dot_split(split(jnp.where(joint, lower[h], 0.0)), parts[h]) for h in each
        ]
        inverse = [inverse[h] - dot_split(parts[h], split(inner[h])) for h in each]
        extent *= 2
    for h in each:
        left = split(inverse[h])
        carry_key = dot_split(left, split(grow[h] * jnp.exp(mid[h])))
        value = v_ref[0, :, lane[h]]
        carry_value = raw_dot(left[0], value) + raw_dot(left[1], value)
        wu = jnp.concatenate([carry_key, carry_value], axis=1)
        wu_ref[h] = wu
        key_end = shrink[h] * jnp.exp(end[h] - mid[h])
        both = dot3(jnp.transpose(key_end) * rate[h], wu)
        ma_ref[h, :, :DK] = eye * jnp.exp(end[h]) - both[:, :DK]
        ma_ref[h, :, DK:] = both[:, DK:]


def maps_call(chunk, keys, values, decay, rate, heads=4):
    steps = CHUNK // heads
    tokens = pl.BlockSpec((1, TOK, heads * DK), lambda i: (0, 0, chunk * steps + i))
    out = pl.BlockSpec((heads, DK, 2 * DK), lambda i: (i, 0, 0))
    shape = jax.ShapeDtypeStruct((CHUNK, DK, 2 * DK), F32)
    return pl.pallas_call(
        functools.partial(maps_kernel, heads),
        grid=(steps,),
        in_specs=[tokens, tokens, tokens, pl.BlockSpec((1, CHUNK, TOK), lambda i: (0, chunk, 0))],
        out_specs=[out, out],
        out_shape=[shape, shape],
        cost_estimate=pl.CostEstimate(flops=2000000000, bytes_accessed=4000000, transcendentals=262144),
        name=f"maps_{chunk}",
    )(keys, values, decay, rate)


def reach_kernel(heads, q_ref, k_ref, g_ref, rate_ref, wu_ref, rb_ref):
    rows, cols = ids(TOK)
    base = pl.program_id(0) * heads
    each = range(heads)
    lane = [slice(h * DK, (h + 1) * DK) for h in each]
    sums = [decay_sums(g_ref[0, :, lane[h]], rows, cols) for h in each]
    mid = [s[TOK // 2 - 1 : TOK // 2, :] for s in sums]
    query = [q_ref[0, :, lane[h]].astype(F32) * jnp.exp(sums[h] - mid[h]) for h in each]
    shrink = [unit_keys(k_ref[0, :, lane[h]]) * jnp.exp(mid[h] - sums[h]) for h in each]
    attend = [dot3(query[h], shrink[h], nt=True) for h in each]
    for h in each:
        rate = rate_ref[0, pl.ds(base + h, 1), :]
        seen = jnp.where(rows >= cols, attend[h] * rate, 0.0)
        both = dot3(seen, wu_ref[h])
        rb_ref[h, :, :DK] = query[h] * jnp.exp(mid[h]) - both[:, :DK]
        rb_ref[h, :, DK:] = both[:, DK:]


def reach_call(chunk, queries, keys, decay, rate, wu, heads=4):
    steps = CHUNK // heads
    tokens = pl.BlockSpec((1, TOK, heads * DK), lambda i: (0, 0, chunk * steps + i))
    pair = pl.BlockSpec((heads, DK, 2 * DK), lambda i: (i, 0, 0))
    return pl.pallas_call(
        functools.partial(reach_kernel, heads),
        grid=(steps,),
        in_specs=[
            tokens,
            tokens,
            tokens,
            pl.BlockSpec((1, CHUNK, TOK), lambda i: (0, chunk, 0)),
            pair,
        ],
        out_specs=pair,
        out_shape=jax.ShapeDtypeStruct((CHUNK, DK, 2 * DK), F32),
        cost_estimate=pl.CostEstimate(flops=600000000, bytes_accessed=4000000, transcendentals=262144),
        name=f"reach_{chunk}",
    )(queries, keys, decay, rate, wu)


def after(late, early):
    both = dot3(late[:, :DK], early)
    return both + jnp.concatenate([jnp.zeros((DK, DK), F32), late[:, DK:]], axis=1)


def total_kernel(parts_ref, total_ref):
    level = [parts_ref[i] for i in range(parts_ref.shape[0])]
    while len(level) > 1:
        level = [after(level[i + 1], level[i]) for i in range(0, len(level), 2)]
    total_ref[...] = level[0]


def prefix_kernel(parts_ref, prefix_ref):
    running = parts_ref[0]
    prefix_ref[0] = running
    for i in range(1, parts_ref.shape[0] - 1):
        running = after(parts_ref[i], running)
        prefix_ref[i] = running


def one_step(kernel, out_shape, flops, name, scalars=0):
    vmem = pl.BlockSpec(memory_space=pltpu.VMEM)
    smem = pl.BlockSpec(memory_space=pltpu.SMEM)

    def call(*args):
        specs = [smem] * scalars + [vmem] * (len(args) - scalars)
        return pl.pallas_call(
            kernel,
            in_specs=specs,
            out_specs=jax.tree.map(lambda _: vmem, out_shape),
            out_shape=out_shape,
            cost_estimate=pl.CostEstimate(flops=flops, bytes_accessed=1000000, transcendentals=0),
            name=name,
        )(*args)

    return call


def pick(refs, place, j):
    back = lax.rem(place - j + len(refs), len(refs))
    value = refs[0][...]
    for s in range(1, len(refs)):
        value = jnp.where(back == s, refs[s][...], value)
    return value


def rows_kernel(place_ref, a, b, c, d, prefix_ref, total_ref):
    place = place_ref[0]
    rows, cols = ids(DK)
    eye = jnp.where(rows == cols, 1.0, 0.0)
    refs = (a, b, c, d)
    prefix = jnp.concatenate([eye, jnp.zeros((DK, DK), F32)], axis=1)
    running = pick(refs, place, 0)
    for j in range(1, 4):
        prefix = jnp.where(place == j, running, prefix)
        running = after(pick(refs, place, j), running)
    prefix_ref[...] = prefix
    total_ref[...] = running


def cores_kernel(place_ref, own_ref, other_ref, total_ref):
    second = place_ref[0] == 1
    own, other = own_ref[...], other_ref[...]
    total_ref[...] = after(jnp.where(second, own, other), jnp.where(second, other, own))


def starts_kernel(place_ref, a, b, c, d, other_ref, rows_ref, prefix_ref, start_ref):
    place, second = place_ref[0], place_ref[1] == 1
    refs = (a, b, c, d)
    state = jnp.zeros((DK, DK), F32)
    for j in range(3):
        part = pick(refs, place, j)
        moved = part[:, DK:]
        if j > 0:
            moved = dot3(part[:, :DK], state) + moved
        state = jnp.where(place > j, moved, state)
    other = other_ref[...]
    state = jnp.where(second, dot3(other[:, :DK], state) + other[:, DK:], state)
    row = rows_ref[...]
    state = dot3(row[:, :DK], state) + row[:, DK:]
    start_ref[0] = state
    halves = split(state)
    for i in range(1, start_ref.shape[0]):
        part = prefix_ref[i - 1]
        start_ref[i] = dot_split(split(part[:, :DK]), halves) + part[:, DK:]


def final_kernel(heads, rb_ref, state_ref, gate_ref, *out):
    out_ref = out[-1]
    for h in range(heads):
        raw = dot3(rb_ref[h, :, :DK], state_ref[h]) + rb_ref[h, :, DK:]
        scaled = raw * lax.rsqrt(jnp.mean(raw * raw, axis=-1, keepdims=True) + 1e-05)
        gate = gate_ref[0, :, h * DK : (h + 1) * DK].astype(F32)
        out_ref[0, :, h * DK : (h + 1) * DK] = (scaled * jax.nn.sigmoid(gate)).astype(BF16)


def final_call(chunk, rb, state, gate, done=None, heads=4):
    steps = CHUNK // heads
    tokens = pl.BlockSpec((1, TOK, heads * DK), lambda i: (0, 0, chunk * steps + i))
    args = [rb, state, gate]
    specs = [
        pl.BlockSpec((heads, TOK, 2 * DK), lambda i: (i, 0, 0)),
        pl.BlockSpec((heads, DK, DK), lambda i: (i, 0, 0)),
        tokens,
    ]
    if done is not None:
        args.append(done)
        specs.append(pl.BlockSpec(memory_space=pl.ANY))
    return pl.pallas_call(
        functools.partial(final_kernel, heads),
        grid=(steps,),
        in_specs=specs,
        out_specs=tokens,
        out_shape=jax.ShapeDtypeStruct(gate.shape, BF16),
        input_output_aliases={} if done is None else {3: 0},
        cost_estimate=pl.CostEstimate(flops=200000000, bytes_accessed=2000000, transcendentals=131072),
        name=f"final_{chunk}",
    )(*args)


def shards(sizes, queries, keys, values, decay, rate, gate):
    depth, width, high, cores = sizes
    seq, grp = lax.axis_index("seq"), lax.axis_index("grp")
    row, column, core = seq // depth, grp // cores, grp % cores
    rings = [[y * depth + z for z in range(depth)] for y in range(width)]
    pair = jax.ShapeDtypeStruct((DK, 2 * DK), F32)
    row_place = row.reshape(1)
    core_place = core.reshape(1)
    place = jnp.stack([column, core])

    def exchanged(x):
        return lax.all_to_all(x, "seq", 0, 0, axis_index_groups=rings, tiled=True)

    def shifted(x, axis, count, inner, step):
        size = count * inner
        return lax.ppermute(x, axis, [(i, (i + step * inner) % size) for i in range(size)])

    maps = [maps_call(c, keys, values, decay, rate) for c in range(2)]
    reach = [reach_call(c, queries, keys, decay, rate, maps[c][1]) for c in range(2)]
    states = []
    for c in range(2):
        parts = exchanged(maps[c][0])
        total = one_step(total_kernel, pair, 200000000, f"total_{c}")(parts)
        prefix = one_step(
            prefix_kernel,
            jax.ShapeDtypeStruct((depth - 1, DK, 2 * DK), F32),
            200000000,
            f"prefix_{c}",
        )(parts)
        others = [shifted(total, "seq", width, depth, s) for s in range(1, width)]
        row_prefix, row_total = one_step(rows_kernel, [pair, pair], 80000000, f"rows_{c}", 1)(
            row_place, total, *others
        )
        other = lax.ppermute(row_total, "grp", [(i, i ^ 1) for i in range(cores * high)])
        chip = one_step(cores_kernel, pair, 30000000, f"cores_{c}", 1)(core_place, row_total, other)
        chips = [shifted(chip, "grp", high, cores, s) for s in range(1, high)]
        starts = one_step(
            starts_kernel,
            jax.ShapeDtypeStruct((depth, DK, DK), F32),
            150000000,
            f"starts_{c}",
            1,
        )(place, chip, *chips, other, row_prefix, prefix)
        states.append(exchanged(starts))
    out = final_call(0, reach[0], states[0], gate)
    return final_call(1, reach[1], states[1], gate, out)


def solution(mesh):
    tokens = P(None, ("grp", "seq"), None)
    placed = (tokens, tokens, tokens, tokens, P(None, None, ("grp", "seq")), tokens)
    sizes = (8, mesh.shape["seq"] // 8, mesh.shape["grp"] // 2, 2)
    return jax.shard_map(
        functools.partial(shards, sizes),
        mesh=mesh,
        in_specs=placed,
        out_specs=tokens,
        check_vma=False,
    )
```

```python
import functools

import jax
import jax.numpy as jnp
from jax import lax
from jax.experimental import pallas as pl
from jax.experimental.pallas import tpu as pltpu
from jax.sharding import PartitionSpec as P

DK = 128
TOK = 128
DEPTH = 8
LOT = 2
WIDE = LOT * DK
SENDS = ((3, 5), (2, 6), (4, 1), (7, 0))
F32 = jnp.float32
BF16 = jnp.bfloat16
MIB = 1 << 20


def split(x):
    hi = x.astype(BF16)
    return hi, (x - hi.astype(F32)).astype(BF16)


def raw_dot(a, b, nt=False):
    dims = (((1,), (1 if nt else 0,)), ((), ()))
    return lax.dot_general(a, b, dims, preferred_element_type=F32)


def dot_split(a, b, nt=False):
    (ah, al), (bh, bl) = a, b
    return raw_dot(ah, bh, nt) + (raw_dot(ah, bl, nt) + raw_dot(al, bh, nt))


def dot3(a, b, nt=False):
    return dot_split(split(a), split(b), nt)


def ids(extent):
    rows = lax.broadcasted_iota(jnp.int32, (extent, extent), 0)
    cols = lax.broadcasted_iota(jnp.int32, (extent, extent), 1)
    return rows, cols


def unit_keys(key):
    key = key.astype(F32)
    return key * lax.rsqrt(jnp.sum(key * key, axis=-1, keepdims=True) + 1e-06)


def decay_sums(decay, rows, cols):
    tri = jnp.where(rows >= cols, 1.0, 0.0).astype(BF16)
    return raw_dot(tri, decay)


def head_views(refs):
    return [ref[0, :, h * DK : (h + 1) * DK] for ref in refs for h in range(LOT)]


def rate_rows(order_ref, rate_ref, shifts):
    return [
        rate_ref[0, pl.ds(order_ref[s] * LOT + h, 1), :] for s in shifts for h in range(LOT)
    ]


def maps_kernel(shifts, order_ref, ka, kb, va, vb, ga, gb, rate_ref, out_a, out_b, wu_ref):
    rows, cols = ids(TOK)
    eye = jnp.where(rows == cols, 1.0, 0.0)
    half = TOK // 2
    rate = rate_rows(order_ref, rate_ref, shifts)
    each = range(len(rate))
    sums = [decay_sums(g, rows, cols) for g in head_views((ga, gb))]
    unit = [unit_keys(k) for k in head_views((ka, kb))]
    values = head_views((va, vb))
    mid = [s[half - 1 : half, :] for s in sums]
    end = [s[TOK - 1 :, :] for s in sums]
    grow = [unit[h] * jnp.exp(sums[h] - mid[h]) for h in each]
    shrink = [unit[h] * jnp.exp(mid[h] - sums[h]) for h in each]
    affinity = [dot3(grow[h], shrink[h], nt=True) * rate[h] for h in each]
    lower = [jnp.where(rows > cols, a, 0.0) for a in affinity]
    apart = rows ^ cols
    one = [-jnp.where(apart < 16, lo, 0.0) for lo in lower]
    one_s = [split(x) for x in one]
    two = [dot_split(x, x) for x in one_s]
    two_s = [split(x) for x in two]
    three = [dot_split(one_s[h], two_s[h]) for h in each]
    four_s = [split(dot_split(x, x)) for x in two_s]
    inverse = [(eye + one[h]) + (two[h] + three[h]) for h in each]
    inverse = [inverse[h] + dot_split(split(inverse[h]), four_s[h]) for h in each]
    eight_s = [split(dot_split(x, x)) for x in four_s]
    inverse = [inverse[h] + dot_split(split(inverse[h]), eight_s[h]) for h in each]
    for extent in (16, 32):
        joint = (apart >= extent) & (apart < 2 * extent)
        parts = [split(inv) for inv in inverse]
        inner = [dot_split(split(jnp.where(joint, lower[h], 0.0)), parts[h]) for h in each]
        inverse = [inverse[h] - dot_split(parts[h], split(inner[h])) for h in each]
    for h in each:
        left = split(inverse[h])
        key_h, key_l = split(grow[h] * jnp.exp(mid[h]))
        carry_key = raw_dot(left[0], key_h) + (raw_dot(left[0], key_l) + raw_dot(left[1], key_h))
        carry_value = raw_dot(left[0], values[h]) + raw_dot(left[1], values[h])
        wu = jnp.concatenate([carry_key, carry_value], axis=1)
        top = wu[:half]
        inner = dot3(lower[h][half:, :half], top)
        corner = tuple(x[half:, half:] for x in left)
        wu = jnp.concatenate([top, wu[half:] - dot_split(corner, split(inner))], axis=0)
        wu_ref[h] = wu
        key_end = shrink[h] * jnp.exp(end[h] - mid[h])
        both = dot3(jnp.transpose(wu) * rate[h], key_end)
        out = (out_a, out_b)[h // LOT]
        out[h % LOT, :DK] = eye * jnp.exp(end[h]) - both[:DK]
        out[h % LOT, DK:] = both[DK:]


def params(mib, **more):
    return pltpu.CompilerParams(vmem_limit_bytes=mib * MIB, **more)


def cost(flops, moved):
    return pl.CostEstimate(flops=flops, bytes_accessed=moved, transcendentals=0)


def token_spec(shift):
    return pl.BlockSpec((1, TOK, WIDE), lambda i, order: (0, 0, order[shift]))


def whole(*shape):
    return pl.BlockSpec(shape, lambda i, order: (0,) * len(shape))


def f32(*shape):
    return jax.ShapeDtypeStruct(shape, F32)


def maps_call(shifts, order, keys, values, decay, rate):
    pair = [token_spec(s) for s in shifts]
    return pl.pallas_call(
        functools.partial(maps_kernel, shifts),
        grid_spec=pltpu.PrefetchScalarGridSpec(
            num_scalar_prefetch=1,
            grid=(1,),
            in_specs=pair * 3 + [whole(*rate.shape)],
            out_specs=[whole(LOT, 2 * DK, DK)] * 2 + [whole(2 * LOT, TOK, 2 * DK)],
        ),
        out_shape=[f32(LOT, 2 * DK, DK)] * 2 + [f32(2 * LOT, TOK, 2 * DK)],
        cost_estimate=cost(1000000000, 1500000),
        compiler_params=params(40),
        name=f"maps_{shifts[0]}",
    )(order, keys, keys, values, values, decay, decay, rate)


def reach_kernel(shifts, order_ref, qa, qb, ka, kb, ga, gb, rate_ref, wu_ref, rb_ref):
    rows, cols = ids(TOK)
    rate = rate_rows(order_ref, rate_ref, shifts)
    each = range(len(rate))
    sums = [decay_sums(g, rows, cols) for g in head_views((ga, gb))]
    mid = [s[TOK // 2 - 1 : TOK // 2, :] for s in sums]
    query = head_views((qa, qb))
    query = [query[h].astype(F32) * jnp.exp(sums[h] - mid[h]) for h in each]
    keys = head_views((ka, kb))
    shrink = [unit_keys(keys[h]) * jnp.exp(mid[h] - sums[h]) for h in each]
    attend = [dot3(query[h], shrink[h], nt=True) for h in each]
    for h in each:
        seen = jnp.where(rows >= cols, attend[h] * rate[h], 0.0)
        both = dot3(seen, wu_ref[h])
        rb_ref[h, :, :DK] = query[h] * jnp.exp(mid[h]) - both[:, :DK]
        rb_ref[h, :, DK:] = both[:, DK:]


def reach_call(shifts, order, queries, keys, decay, rate, wu):
    pair = [token_spec(s) for s in shifts]
    return pl.pallas_call(
        functools.partial(reach_kernel, shifts),
        grid_spec=pltpu.PrefetchScalarGridSpec(
            num_scalar_prefetch=1,
            grid=(1,),
            in_specs=pair * 3 + [whole(*rate.shape), whole(*wu.shape)],
            out_specs=whole(2 * LOT, TOK, 2 * DK),
        ),
        out_shape=f32(2 * LOT, TOK, 2 * DK),
        cost_estimate=cost(300000000, 2000000),
        compiler_params=params(40),
        name=f"reach_{shifts[0]}",
    )(order, queries, queries, keys, keys, decay, decay, rate, wu)


def one_step(kernel, out_shape, flops, name, scratch=()):
    vmem = pl.BlockSpec(memory_space=pltpu.VMEM)

    def call(*args):
        return pl.pallas_call(
            kernel,
            in_specs=[vmem] * len(args),
            out_specs=jax.tree.map(lambda _: vmem, out_shape),
            out_shape=out_shape,
            scratch_shapes=scratch,
            cost_estimate=cost(flops, 1000000),
            compiler_params=params(16),
            name=name,
        )(*args)

    return call


def along():
    return lax.rem(lax.axis_index("seq"), DEPTH)


def after(late, early):
    both = dot3(early, late[:DK])
    return jnp.concatenate([both[:DK], both[DK:] + late[DK:]], axis=0)


def moved(state, part):
    return dot3(state, part[:DK]) + part[DK:]


def parts_kernel(*refs):
    ins, (all_ref, tree_ref, total_ref) = refs[:DEPTH], refs[DEPTH:]
    place = along()
    for s in range(DEPTH):
        all_ref[lax.rem(place - s + DEPTH, DEPTH)] = ins[s][...]
    for h in range(LOT):
        pairs = [after(all_ref[2 * i + 1, h], all_ref[2 * i, h]) for i in range(4)]
        quads = [after(pairs[1], pairs[0]), after(pairs[3], pairs[2])]
        tree_ref[0, h] = pairs[0]
        tree_ref[1, h] = pairs[2]
        tree_ref[2, h] = quads[0]
        total_ref[h] = after(quads[1], quads[0])


def picked(refs, index, h):
    value = refs[0][h]
    for s in range(1, len(refs)):
        value = jnp.where(index == s, refs[s][h], value)
    return value


def rows_kernel(a, b, c, d, prefix_ref, total_ref):
    row = lax.axis_index("seq") // DEPTH
    rows, cols = ids(DK)
    eye = jnp.where(rows == cols, 1.0, 0.0)
    blank = jnp.concatenate([eye, jnp.zeros((DK, DK), F32)], axis=0)
    refs = (a, b, c, d)
    for h in range(LOT):
        prefix = blank
        running = picked(refs, row, h)
        for j in range(1, 4):
            prefix = jnp.where(row == j, running, prefix)
            running = after(picked(refs, row ^ j, h), running)
        prefix_ref[h] = prefix
        total_ref[h] = running


def cores_kernel(own_ref, other_ref, total_ref):
    second = lax.rem(lax.axis_index("grp"), 2) == 1
    for h in range(LOT):
        own, other = own_ref[h], other_ref[h]
        total_ref[h] = after(jnp.where(second, own, other), jnp.where(second, other, own))


def entry_kernel(prefix_ref, other_ref, entry_ref):
    second = lax.rem(lax.axis_index("grp"), 2) == 1
    for h in range(LOT):
        prefix = prefix_ref[h]
        entry_ref[h] = jnp.where(second, after(prefix, other_ref[h]), prefix)


def starts_kernel(a, b, c, d, entry_ref, all_ref, tree_ref, *refs):
    outs, state_ref = refs[:DEPTH], refs[DEPTH]
    column = lax.axis_index("grp") // 2
    columns = (a, b, c, d)
    for h in range(LOT):
        state = jnp.zeros((DK, DK), F32)
        for j in range(3):
            part = picked(columns, column ^ j, h)
            following = part[DK:] if j == 0 else moved(state, part)
            state = jnp.where(column > j, following, state)
        states = [None] * DEPTH
        states[0] = moved(state, entry_ref[h])
        states[4] = moved(states[0], tree_ref[2, h])
        states[2] = moved(states[0], tree_ref[0, h])
        states[6] = moved(states[4], tree_ref[1, h])
        for i in (0, 2, 4, 6):
            states[i + 1] = moved(states[i], all_ref[i, h])
        for i in range(DEPTH):
            state_ref[i, h] = states[i]
    place = along()
    for s in range(DEPTH):
        outs[s][...] = state_ref[lax.rem(place + s, DEPTH)]


def final_kernel(order_ref, rb_ref, gate_ref, sa, sb, *refs):
    out_ref = refs[-1]

    def head_out(state_ref):
        for h in range(LOT):
            raw = dot3(rb_ref[h, :, :DK], state_ref[h], nt=True) + rb_ref[h, :, DK:]
            scaled = raw * lax.rsqrt(jnp.mean(raw * raw, axis=-1, keepdims=True) + 1e-05)
            gate = gate_ref[0, :, h * DK : (h + 1) * DK].astype(F32)
            out_ref[0, :, h * DK : (h + 1) * DK] = (scaled * jax.nn.sigmoid(gate)).astype(BF16)

    for step, state_ref in enumerate((sa, sb)):

        @pl.when(pl.program_id(0) == step)
        def _(state_ref=state_ref):
            head_out(state_ref)


def final_call(shifts, order, rb, gate, states, done=None):
    first, second = shifts

    def tokens(i, order):
        return 0, 0, jnp.where(i == 0, order[first], order[second])

    args = [rb, gate, *states]
    specs = [
        pl.BlockSpec((LOT, TOK, 2 * DK), lambda i, order: (i, 0, 0)),
        pl.BlockSpec((1, TOK, WIDE), tokens),
        whole(LOT, DK, DK),
        whole(LOT, DK, DK),
    ]
    if done is not None:
        args.append(done)
        specs.append(pl.BlockSpec(memory_space=pl.ANY))
    return pl.pallas_call(
        final_kernel,
        grid_spec=pltpu.PrefetchScalarGridSpec(
            num_scalar_prefetch=1,
            grid=(2,),
            in_specs=specs,
            out_specs=pl.BlockSpec((1, TOK, WIDE), tokens),
        ),
        out_shape=jax.ShapeDtypeStruct(gate.shape, BF16),
        input_output_aliases={} if done is None else {5: 0},
        cost_estimate=cost(100000000, 1000000),
        compiler_params=params(40),
        name=f"final_{first}",
    )(order, *args)


def shards(groups, queries, keys, values, decay, rate, gate):
    order = lax.rem(along() + jnp.arange(DEPTH, dtype=jnp.int32), DEPTH)
    size = lax.axis_size("seq")
    lot = f32(LOT, 2 * DK, DK)

    def turned(x, s):
        perm = [(i, i // DEPTH * DEPTH + (i + s) % DEPTH) for i in range(size)]
        return lax.ppermute(x, "seq", perm) if s else x

    def crossed(x, axis, count, inner):
        return [x] + [
            lax.ppermute(x, axis, [(i, i ^ (flip * inner)) for i in range(count)])
            for flip in (1, 2, 3)
        ]

    carried, got = [], [None] * DEPTH
    for shifts in SENDS:
        first, second, wu = maps_call(shifts, order, keys, values, decay, rate)
        got[shifts[0]] = turned(first, shifts[0])
        got[shifts[1]] = turned(second, shifts[1])
        carried.append(wu)
    reach = [
        reach_call(s, order, queries, keys, decay, rate, wu) for s, wu in zip(SENDS, carried)
    ]
    parts, tree, total = one_step(
        parts_kernel,
        [f32(DEPTH, LOT, 2 * DK, DK), f32(3, LOT, 2 * DK, DK), lot],
        300000000,
        "parts",
    )(*got)
    prefix, total = one_step(rows_kernel, [lot, lot], 100000000, "rows")(
        *crossed(total, "seq", size, DEPTH)
    )
    other = lax.ppermute(total, "grp", [(i, i ^ 1) for i in range(groups)])
    total = one_step(cores_kernel, lot, 40000000, "cores")(total, other)
    columns = crossed(total, "grp", groups, 2)
    entry = one_step(entry_kernel, lot, 40000000, "entry")(prefix, other)
    starts = one_step(
        starts_kernel,
        [f32(LOT, DK, DK)] * DEPTH,
        150000000,
        "starts",
        [pltpu.VMEM((DEPTH, LOT, DK, DK), F32)],
    )(*columns, entry, parts, tree)
    states = [None] * DEPTH
    for s in (3, 5, 2, 6, 4, 1, 7, 0):
        states[-s % DEPTH] = turned(starts[s], s)
    out = None
    for k in (0, 1, 2, 3):
        shifts = SENDS[k]
        out = final_call(shifts, order, reach[k], gate, [states[s] for s in shifts], out)
    return out


def solution(mesh):
    tokens = P(None, ("grp", "seq"), None)
    placed = (tokens, tokens, tokens, tokens, P(None, None, ("grp", "seq")), tokens)
    return jax.shard_map(
        functools.partial(shards, mesh.shape["grp"]),
        mesh=mesh,
        in_specs=placed,
        out_specs=tokens,
        check_vma=False,
    )
```

```python
import functools

import jax
import jax.numpy as jnp
from jax import lax
from jax.experimental import pallas as pl
from jax.experimental.pallas import tpu as pltpu
from jax.sharding import PartitionSpec as P

DK = 128
TOK = 128
DEPTH = 8
LOT = 2
WIDE = LOT * DK
SENDS = ((3, 5), (2, 6), (4, 1), (7, 0))
F32 = jnp.float32
BF16 = jnp.bfloat16
MIB = 1 << 20


def split(x):
    hi = x.astype(BF16)
    return hi, (x - hi.astype(F32)).astype(BF16)


def raw_dot(a, b, nt=False):
    dims = (((1,), (1 if nt else 0,)), ((), ()))
    return lax.dot_general(a, b, dims, preferred_element_type=F32)


def dot_split(a, b, nt=False):
    (ah, al), (bh, bl) = a, b
    return raw_dot(ah, bh, nt) + (raw_dot(ah, bl, nt) + raw_dot(al, bh, nt))


def dot3(a, b, nt=False):
    return dot_split(split(a), split(b), nt)


def ids(extent):
    rows = lax.broadcasted_iota(jnp.int32, (extent, extent), 0)
    cols = lax.broadcasted_iota(jnp.int32, (extent, extent), 1)
    return rows, cols


def unit_keys(key):
    key = key.astype(F32)
    return key * lax.rsqrt(jnp.sum(key * key, axis=-1, keepdims=True) + 1e-06)


def decay_sums(decay, rows, cols):
    tri = jnp.where(rows >= cols, 1.0, 0.0).astype(BF16)
    return raw_dot(tri, decay)


def head_views(refs):
    return [ref[0, :, h * DK : (h + 1) * DK] for ref in refs for h in range(LOT)]


def rate_rows(order_ref, rate_ref, shifts):
    return [
        rate_ref[0, pl.ds(order_ref[s] * LOT + h, 1), :] for s in shifts for h in range(LOT)
    ]


def maps_kernel(shifts, order_ref, ka, kb, va, vb, ga, gb, rate_ref, out_a, out_b, wu_ref):
    rows, cols = ids(TOK)
    eye = jnp.where(rows == cols, 1.0, 0.0)
    half = TOK // 2
    rate = rate_rows(order_ref, rate_ref, shifts)
    each = range(len(rate))
    sums = [decay_sums(g, rows, cols) for g in head_views((ga, gb))]
    unit = [unit_keys(k) for k in head_views((ka, kb))]
    values = head_views((va, vb))
    mid = [s[half - 1 : half, :] for s in sums]
    end = [s[TOK - 1 :, :] for s in sums]
    grow = [unit[h] * jnp.exp(sums[h] - mid[h]) for h in each]
    shrink = [unit[h] * jnp.exp(mid[h] - sums[h]) for h in each]
    affinity = [dot3(grow[h], shrink[h], nt=True) * rate[h] for h in each]
    lower = [jnp.where(rows > cols, a, 0.0) for a in affinity]
    apart = rows ^ cols
    one = [-jnp.where(apart < 16, lo, 0.0) for lo in lower]
    one_s = [split(x) for x in one]
    two = [dot_split(x, x) for x in one_s]
    two_s = [split(x) for x in two]
    three = [dot_split(one_s[h], two_s[h]) for h in each]
    four_s = [split(dot_split(x, x)) for x in two_s]
    inverse = [(eye + one[h]) + (two[h] + three[h]) for h in each]
    inverse = [inverse[h] + dot_split(split(inverse[h]), four_s[h]) for h in each]
    eight_s = [split(dot_split(x, x)) for x in four_s]
    inverse = [inverse[h] + dot_split(split(inverse[h]), eight_s[h]) for h in each]
    for extent in (16, 32):
        joint = (apart >= extent) & (apart < 2 * extent)
        parts = [split(inv) for inv in inverse]
        inner = [dot_split(split(jnp.where(joint, lower[h], 0.0)), parts[h]) for h in each]
        inverse = [inverse[h] - dot_split(parts[h], split(inner[h])) for h in each]
    for h in each:
        left = split(inverse[h])
        key_h, key_l = split(grow[h] * jnp.exp(mid[h]))
        carry_key = raw_dot(left[0], key_h) + (raw_dot(left[0], key_l) + raw_dot(left[1], key_h))
        carry_value = raw_dot(left[0], values[h]) + raw_dot(left[1], values[h])
        wu = jnp.concatenate([carry_key, carry_value], axis=1)
        top = wu[:half]
        inner = dot3(lower[h][half:, :half], top)
        corner = tuple(x[half:, half:] for x in left)
        wu = jnp.concatenate([top, wu[half:] - dot_split(corner, split(inner))], axis=0)
        wu_ref[h] = wu
        key_end = shrink[h] * jnp.exp(end[h] - mid[h])
        both = dot3(jnp.transpose(wu) * rate[h], key_end)
        out = (out_a, out_b)[h // LOT]
        out[h % LOT, :DK] = eye * jnp.exp(end[h]) - both[:DK]
        out[h % LOT, DK:] = both[DK:]


def params(mib, **more):
    return pltpu.CompilerParams(vmem_limit_bytes=mib * MIB, **more)


def cost(flops, moved):
    return pl.CostEstimate(flops=flops, bytes_accessed=moved, transcendentals=0)


def token_spec(shift):
    return pl.BlockSpec((1, TOK, WIDE), lambda i, order: (0, 0, order[shift]))


def whole(*shape):
    return pl.BlockSpec(shape, lambda i, order: (0,) * len(shape))


def f32(*shape):
    return jax.ShapeDtypeStruct(shape, F32)


def maps_call(shifts, order, keys, values, decay, rate):
    pair = [token_spec(s) for s in shifts]
    return pl.pallas_call(
        functools.partial(maps_kernel, shifts),
        grid_spec=pltpu.PrefetchScalarGridSpec(
            num_scalar_prefetch=1,
            grid=(1,),
            in_specs=pair * 3 + [whole(*rate.shape)],
            out_specs=[whole(LOT, 2 * DK, DK)] * 2 + [whole(2 * LOT, TOK, 2 * DK)],
        ),
        out_shape=[f32(LOT, 2 * DK, DK)] * 2 + [f32(2 * LOT, TOK, 2 * DK)],
        cost_estimate=cost(1000000000, 1500000),
        compiler_params=params(60 if shifts == SENDS[0] else 40),
        name=f"maps_{shifts[0]}",
    )(order, keys, keys, values, values, decay, decay, rate)


def reach_kernel(shifts, order_ref, qa, qb, ka, kb, ga, gb, rate_ref, wu_ref, rb_ref):
    rows, cols = ids(TOK)
    rate = rate_rows(order_ref, rate_ref, shifts)
    each = range(len(rate))
    sums = [decay_sums(g, rows, cols) for g in head_views((ga, gb))]
    mid = [s[TOK // 2 - 1 : TOK // 2, :] for s in sums]
    query = head_views((qa, qb))
    query = [query[h].astype(F32) * jnp.exp(sums[h] - mid[h]) for h in each]
    keys = head_views((ka, kb))
    shrink = [unit_keys(keys[h]) * jnp.exp(mid[h] - sums[h]) for h in each]
    attend = [dot3(query[h], shrink[h], nt=True) for h in each]
    for h in each:
        seen = jnp.where(rows >= cols, attend[h] * rate[h], 0.0)
        both = dot3(seen, wu_ref[h])
        rb_ref[h, :, :DK] = query[h] * jnp.exp(mid[h]) - both[:, :DK]
        rb_ref[h, :, DK:] = both[:, DK:]


def reach_call(shifts, order, queries, keys, decay, rate, wu):
    pair = [token_spec(s) for s in shifts]
    return pl.pallas_call(
        functools.partial(reach_kernel, shifts),
        grid_spec=pltpu.PrefetchScalarGridSpec(
            num_scalar_prefetch=1,
            grid=(1,),
            in_specs=pair * 3 + [whole(*rate.shape), whole(*wu.shape)],
            out_specs=whole(2 * LOT, TOK, 2 * DK),
        ),
        out_shape=f32(2 * LOT, TOK, 2 * DK),
        cost_estimate=cost(300000000, 2000000),
        compiler_params=params(40),
        name=f"reach_{shifts[0]}",
    )(order, queries, queries, keys, keys, decay, decay, rate, wu)


def one_step(kernel, out_shape, flops, name, scratch=()):
    vmem = pl.BlockSpec(memory_space=pltpu.VMEM)

    def call(*args):
        return pl.pallas_call(
            kernel,
            in_specs=[vmem] * len(args),
            out_specs=jax.tree.map(lambda _: vmem, out_shape),
            out_shape=out_shape,
            scratch_shapes=scratch,
            cost_estimate=cost(flops, 1000000),
            compiler_params=params(16),
            name=name,
        )(*args)

    return call


def along():
    return lax.rem(lax.axis_index("seq"), DEPTH)


def after(late, early):
    both = dot3(early, late[:DK])
    return jnp.concatenate([both[:DK], both[DK:] + late[DK:]], axis=0)


def moved(state, part):
    return dot3(state, part[:DK]) + part[DK:]


def parts_kernel(*refs):
    ins, (all_ref, tree_ref, total_ref) = refs[:DEPTH], refs[DEPTH:]
    place = along()
    for s in range(DEPTH):
        all_ref[lax.rem(place - s + DEPTH, DEPTH)] = ins[s][...]
    for h in range(LOT):
        pairs = [after(all_ref[2 * i + 1, h], all_ref[2 * i, h]) for i in range(4)]
        quads = [after(pairs[1], pairs[0]), after(pairs[3], pairs[2])]
        tree_ref[0, h] = pairs[0]
        tree_ref[1, h] = pairs[2]
        tree_ref[2, h] = quads[0]
        total_ref[h] = after(quads[1], quads[0])


def picked(refs, index, h):
    value = refs[0][h]
    for s in range(1, len(refs)):
        value = jnp.where(index == s, refs[s][h], value)
    return value


def rows_kernel(a, b, c, d, prefix_ref, total_ref):
    row = lax.axis_index("seq") // DEPTH
    rows, cols = ids(DK)
    eye = jnp.where(rows == cols, 1.0, 0.0)
    blank = jnp.concatenate([eye, jnp.zeros((DK, DK), F32)], axis=0)
    refs = (a, b, c, d)
    for h in range(LOT):
        prefix = blank
        running = picked(refs, row, h)
        for j in range(1, 4):
            prefix = jnp.where(row == j, running, prefix)
            running = after(picked(refs, row ^ j, h), running)
        prefix_ref[h] = prefix
        total_ref[h] = running


def cores_kernel(own_ref, other_ref, total_ref):
    second = lax.rem(lax.axis_index("grp"), 2) == 1
    for h in range(LOT):
        own, other = own_ref[h], other_ref[h]
        total_ref[h] = after(jnp.where(second, own, other), jnp.where(second, other, own))


def entry_kernel(prefix_ref, other_ref, entry_ref):
    second = lax.rem(lax.axis_index("grp"), 2) == 1
    for h in range(LOT):
        prefix = prefix_ref[h]
        entry_ref[h] = jnp.where(second, after(prefix, other_ref[h]), prefix)


def starts_kernel(a, b, c, d, entry_ref, all_ref, tree_ref, *refs):
    outs, state_ref = refs[:DEPTH], refs[DEPTH]
    column = lax.axis_index("grp") // 2
    columns = (a, b, c, d)
    for h in range(LOT):
        state = jnp.zeros((DK, DK), F32)
        for j in range(3):
            part = picked(columns, column ^ j, h)
            following = part[DK:] if j == 0 else moved(state, part)
            state = jnp.where(column > j, following, state)
        states = [None] * DEPTH
        states[0] = moved(state, entry_ref[h])
        states[4] = moved(states[0], tree_ref[2, h])
        states[2] = moved(states[0], tree_ref[0, h])
        states[6] = moved(states[4], tree_ref[1, h])
        for i in (0, 2, 4, 6):
            states[i + 1] = moved(states[i], all_ref[i, h])
        for i in range(DEPTH):
            state_ref[i, h] = states[i]
    place = along()
    for s in range(DEPTH):
        outs[s][...] = state_ref[lax.rem(place + s, DEPTH)]


def final_kernel(order_ref, rb_ref, gate_ref, sa, sb, *refs):
    out_ref = refs[-1]

    def head_out(state_ref):
        for h in range(LOT):
            raw = dot3(rb_ref[h, :, :DK], state_ref[h], nt=True) + rb_ref[h, :, DK:]
            scaled = raw * lax.rsqrt(jnp.mean(raw * raw, axis=-1, keepdims=True) + 1e-05)
            gate = gate_ref[0, :, h * DK : (h + 1) * DK].astype(F32)
            out_ref[0, :, h * DK : (h + 1) * DK] = (scaled * jax.nn.sigmoid(gate)).astype(BF16)

    for step, state_ref in enumerate((sa, sb)):

        @pl.when(pl.program_id(0) == step)
        def _(state_ref=state_ref):
            head_out(state_ref)


def final_call(shifts, order, rb, gate, states, done=None):
    first, second = shifts

    def tokens(i, order):
        return 0, 0, jnp.where(i == 0, order[first], order[second])

    args = [rb, gate, *states]
    specs = [
        pl.BlockSpec((LOT, TOK, 2 * DK), lambda i, order: (i, 0, 0)),
        pl.BlockSpec((1, TOK, WIDE), tokens),
        whole(LOT, DK, DK),
        whole(LOT, DK, DK),
    ]
    if done is not None:
        args.append(done)
        specs.append(pl.BlockSpec(memory_space=pl.ANY))
    return pl.pallas_call(
        final_kernel,
        grid_spec=pltpu.PrefetchScalarGridSpec(
            num_scalar_prefetch=1,
            grid=(2,),
            in_specs=specs,
            out_specs=pl.BlockSpec((1, TOK, WIDE), tokens),
        ),
        out_shape=jax.ShapeDtypeStruct(gate.shape, BF16),
        input_output_aliases={} if done is None else {5: 0},
        cost_estimate=cost(100000000, 1000000),
        compiler_params=params(40),
        name=f"final_{first}",
    )(order, *args)


def shards(groups, queries, keys, values, decay, rate, gate):
    order = lax.rem(along() + jnp.arange(DEPTH, dtype=jnp.int32), DEPTH)
    size = lax.axis_size("seq")
    lot = f32(LOT, 2 * DK, DK)

    def turned(x, s):
        perm = [(i, i // DEPTH * DEPTH + (i + s) % DEPTH) for i in range(size)]
        return lax.ppermute(x, "seq", perm) if s else x

    def crossed(x, axis, count, inner):
        return [x] + [
            lax.ppermute(x, axis, [(i, i ^ (flip * inner)) for i in range(count)])
            for flip in (1, 2, 3)
        ]

    carried, got, turn = [], [None] * DEPTH, order
    for shifts in SENDS:
        first, second, wu = maps_call(shifts, turn, keys, values, decay, rate)
        turn, first, second, wu = lax.optimization_barrier((turn, first, second, wu))
        got[shifts[0]] = turned(first, shifts[0])
        got[shifts[1]] = turned(second, shifts[1])
        carried.append(wu)
    reach = [
        reach_call(s, order, queries, keys, decay, rate, wu) for s, wu in zip(SENDS, carried)
    ]
    parts, tree, total = one_step(
        parts_kernel,
        [f32(DEPTH, LOT, 2 * DK, DK), f32(3, LOT, 2 * DK, DK), lot],
        300000000,
        "parts",
    )(*got)
    prefix, total = one_step(rows_kernel, [lot, lot], 100000000, "rows")(
        *crossed(total, "seq", size, DEPTH)
    )
    other = lax.ppermute(total, "grp", [(i, i ^ 1) for i in range(groups)])
    total = one_step(cores_kernel, lot, 40000000, "cores")(total, other)
    columns = crossed(total, "grp", groups, 2)
    entry = one_step(entry_kernel, lot, 40000000, "entry")(prefix, other)
    *columns, reach = lax.optimization_barrier((*columns, reach))
    starts = one_step(
        starts_kernel,
        [f32(LOT, DK, DK)] * DEPTH,
        150000000,
        "starts",
        [pltpu.VMEM((DEPTH, LOT, DK, DK), F32)],
    )(*columns, entry, parts, tree)
    states = [None] * DEPTH
    for s in (3, 5, 2, 6, 4, 1, 7, 0):
        states[-s % DEPTH] = turned(starts[s], s)
    out = None
    for k in (0, 1, 2, 3):
        shifts = SENDS[k]
        out = final_call(shifts, order, reach[k], gate, [states[s] for s in shifts], out)
    return out


def solution(mesh):
    tokens = P(None, ("grp", "seq"), None)
    placed = (tokens, tokens, tokens, tokens, P(None, None, ("grp", "seq")), tokens)
    return jax.shard_map(
        functools.partial(shards, mesh.shape["grp"]),
        mesh=mesh,
        in_specs=placed,
        out_specs=tokens,
        check_vma=False,
    )
```

```python
import functools

import jax
import jax.numpy as jnp
from jax import lax
from jax.experimental import pallas as pl
from jax.experimental.pallas import tpu as pltpu
from jax.sharding import PartitionSpec as P

DK = 128
TOK = 128
DEPTH = 8
LOT = 2
WIDE = LOT * DK
SENDS = ((3, 5), (2, 6), (4, 1), (7, 0))
F32 = jnp.float32
BF16 = jnp.bfloat16
MIB = 1 << 20


def split(x):
    hi = x.astype(BF16)
    return hi, (x - hi.astype(F32)).astype(BF16)


def raw_dot(a, b, nt=False):
    dims = (((1,), (1 if nt else 0,)), ((), ()))
    return lax.dot_general(a, b, dims, preferred_element_type=F32)


def dot_split(a, b, nt=False):
    (ah, al), (bh, bl) = a, b
    return raw_dot(ah, bh, nt) + (raw_dot(ah, bl, nt) + raw_dot(al, bh, nt))


def dot3(a, b, nt=False):
    return dot_split(split(a), split(b), nt)


def ids(extent):
    rows = lax.broadcasted_iota(jnp.int32, (extent, extent), 0)
    cols = lax.broadcasted_iota(jnp.int32, (extent, extent), 1)
    return rows, cols


def unit_keys(key):
    key = key.astype(F32)
    return key * lax.rsqrt(jnp.sum(key * key, axis=-1, keepdims=True) + 1e-06)


def decay_sums(decay, rows, cols):
    tri = jnp.where(rows >= cols, 1.0, 0.0).astype(BF16)
    return raw_dot(tri, decay)


def head_views(refs):
    return [ref[0, :, h * DK : (h + 1) * DK] for ref in refs for h in range(LOT)]


def rate_rows(rate_ref, shifts):
    return [
        rate_ref[0, pl.ds(block_of(s) * LOT + h, 1), :] for s in shifts for h in range(LOT)
    ]


def maps_kernel(shifts, ka, kb, va, vb, ga, gb, rate_ref, out_a, out_b, wu_ref):
    rows, cols = ids(TOK)
    eye = jnp.where(rows == cols, 1.0, 0.0)
    half = TOK // 2
    rate = rate_rows(rate_ref, shifts)
    each = range(len(rate))
    sums = [decay_sums(g, rows, cols) for g in head_views((ga, gb))]
    unit = [unit_keys(k) for k in head_views((ka, kb))]
    values = head_views((va, vb))
    mid = [s[half - 1 : half, :] for s in sums]
    end = [s[TOK - 1 :, :] for s in sums]
    grow = [unit[h] * jnp.exp(sums[h] - mid[h]) for h in each]
    shrink = [unit[h] * jnp.exp(mid[h] - sums[h]) for h in each]
    affinity = [dot3(grow[h], shrink[h], nt=True) * rate[h] for h in each]
    lower = [jnp.where(rows > cols, a, 0.0) for a in affinity]
    apart = rows ^ cols
    one = [-jnp.where(apart < 16, lo, 0.0) for lo in lower]
    one_s = [split(x) for x in one]
    two = [dot_split(x, x) for x in one_s]
    two_s = [split(x) for x in two]
    three = [dot_split(one_s[h], two_s[h]) for h in each]
    four_s = [split(dot_split(x, x)) for x in two_s]
    inverse = [(eye + one[h]) + (two[h] + three[h]) for h in each]
    inverse = [inverse[h] + dot_split(split(inverse[h]), four_s[h]) for h in each]
    eight_s = [split(dot_split(x, x)) for x in four_s]
    inverse = [inverse[h] + dot_split(split(inverse[h]), eight_s[h]) for h in each]
    for extent in (16, 32):
        joint = (apart >= extent) & (apart < 2 * extent)
        parts = [split(inv) for inv in inverse]
        inner = [dot_split(split(jnp.where(joint, lower[h], 0.0)), parts[h]) for h in each]
        inverse = [inverse[h] - dot_split(parts[h], split(inner[h])) for h in each]
    for h in each:
        left = split(inverse[h])
        key_h, key_l = split(grow[h] * jnp.exp(mid[h]))
        carry_key = raw_dot(left[0], key_h) + (raw_dot(left[0], key_l) + raw_dot(left[1], key_h))
        carry_value = raw_dot(left[0], values[h]) + raw_dot(left[1], values[h])
        wu = jnp.concatenate([carry_key, carry_value], axis=1)
        top = wu[:half]
        inner = dot3(lower[h][half:, :half], top)
        corner = tuple(x[half:, half:] for x in left)
        wu = jnp.concatenate([top, wu[half:] - dot_split(corner, split(inner))], axis=0)
        wu_ref[h] = wu
        key_end = shrink[h] * jnp.exp(end[h] - mid[h])
        both = dot3(jnp.transpose(wu) * rate[h], key_end)
        out = (out_a, out_b)[h // LOT]
        out[h % LOT, :DK] = eye * jnp.exp(end[h]) - both[:DK]
        out[h % LOT, DK:] = both[DK:]


def params(mib, **more):
    return pltpu.CompilerParams(vmem_limit_bytes=mib * MIB, **more)


def cost(flops, moved):
    return pl.CostEstimate(flops=flops, bytes_accessed=moved, transcendentals=0)


def token_spec(shift):
    return pl.BlockSpec((1, TOK, WIDE), lambda i: (0, 0, block_of(shift)))


def whole(*shape):
    return pl.BlockSpec(shape, lambda i: (0,) * len(shape))


def f32(*shape):
    return jax.ShapeDtypeStruct(shape, F32)


def maps_call(shifts, keys, values, decay, rate):
    pair = [token_spec(s) for s in shifts]
    return pl.pallas_call(
        functools.partial(maps_kernel, shifts),
        grid_spec=pl.GridSpec(
            grid=(1,),
            in_specs=pair * 3 + [whole(*rate.shape)],
            out_specs=[whole(LOT, 2 * DK, DK)] * 2 + [whole(2 * LOT, TOK, 2 * DK)],
        ),
        out_shape=[f32(LOT, 2 * DK, DK)] * 2 + [f32(2 * LOT, TOK, 2 * DK)],
        cost_estimate=cost(1000000000, 1500000),
        compiler_params=params(60 if shifts == SENDS[0] else 40),
        name=f"maps_{shifts[0]}",
    )(keys, keys, values, values, decay, decay, rate)


def reach_kernel(shifts, qa, qb, ka, kb, ga, gb, rate_ref, wu_ref, rb_ref):
    rows, cols = ids(TOK)
    rate = rate_rows(rate_ref, shifts)
    each = range(len(rate))
    sums = [decay_sums(g, rows, cols) for g in head_views((ga, gb))]
    mid = [s[TOK // 2 - 1 : TOK // 2, :] for s in sums]
    query = head_views((qa, qb))
    query = [query[h].astype(F32) * jnp.exp(sums[h] - mid[h]) for h in each]
    keys = head_views((ka, kb))
    shrink = [unit_keys(keys[h]) * jnp.exp(mid[h] - sums[h]) for h in each]
    attend = [dot3(query[h], shrink[h], nt=True) for h in each]
    for h in each:
        seen = jnp.where(rows >= cols, attend[h] * rate[h], 0.0)
        both = dot3(seen, wu_ref[h])
        rb_ref[h, :, :DK] = query[h] * jnp.exp(mid[h]) - both[:, :DK]
        rb_ref[h, :, DK:] = both[:, DK:]


def reach_call(shifts, queries, keys, decay, rate, wu):
    pair = [token_spec(s) for s in shifts]
    return pl.pallas_call(
        functools.partial(reach_kernel, shifts),
        grid_spec=pl.GridSpec(
            grid=(1,),
            in_specs=pair * 3 + [whole(*rate.shape), whole(*wu.shape)],
            out_specs=whole(2 * LOT, TOK, 2 * DK),
        ),
        out_shape=f32(2 * LOT, TOK, 2 * DK),
        cost_estimate=cost(300000000, 2000000),
        compiler_params=params(40),
        name=f"reach_{shifts[0]}",
    )(queries, queries, keys, keys, decay, decay, rate, wu)


def one_step(kernel, out_shape, flops, name, scratch=()):
    vmem = pl.BlockSpec(memory_space=pltpu.VMEM)

    def call(*args):
        return pl.pallas_call(
            kernel,
            in_specs=[vmem] * len(args),
            out_specs=jax.tree.map(lambda _: vmem, out_shape),
            out_shape=out_shape,
            scratch_shapes=scratch,
            cost_estimate=cost(flops, 1000000),
            compiler_params=params(16),
            name=name,
        )(*args)

    return call


def block_of(shift):
    return lax.rem(along() + shift, DEPTH)


def along():
    return lax.rem(lax.axis_index("seq"), DEPTH)


def after(late, early):
    both = dot3(early, late[:DK])
    return jnp.concatenate([both[:DK], both[DK:] + late[DK:]], axis=0)


def moved(state, part):
    return dot3(state, part[:DK]) + part[DK:]


def parts_kernel(*refs):
    ins, (all_ref, tree_ref, total_ref) = refs[:DEPTH], refs[DEPTH:]
    place = along()
    for s in range(DEPTH):
        all_ref[lax.rem(place - s + DEPTH, DEPTH)] = ins[s][...]
    for h in range(LOT):
        pairs = [after(all_ref[2 * i + 1, h], all_ref[2 * i, h]) for i in range(4)]
        quads = [after(pairs[1], pairs[0]), after(pairs[3], pairs[2])]
        tree_ref[0, h] = pairs[0]
        tree_ref[1, h] = pairs[2]
        tree_ref[2, h] = quads[0]
        total_ref[h] = after(quads[1], quads[0])


def picked(refs, index, h):
    value = refs[0][h]
    for s in range(1, len(refs)):
        value = jnp.where(index == s, refs[s][h], value)
    return value


def rows_kernel(a, b, c, d, prefix_ref, total_ref):
    row = lax.axis_index("seq") // DEPTH
    rows, cols = ids(DK)
    eye = jnp.where(rows == cols, 1.0, 0.0)
    blank = jnp.concatenate([eye, jnp.zeros((DK, DK), F32)], axis=0)
    refs = (a, b, c, d)
    for h in range(LOT):
        prefix = blank
        running = picked(refs, row, h)
        for j in range(1, 4):
            prefix = jnp.where(row == j, running, prefix)
            running = after(picked(refs, row ^ j, h), running)
        prefix_ref[h] = prefix
        total_ref[h] = running


def cores_kernel(own_ref, other_ref, total_ref):
    second = lax.rem(lax.axis_index("grp"), 2) == 1
    for h in range(LOT):
        own, other = own_ref[h], other_ref[h]
        total_ref[h] = after(jnp.where(second, own, other), jnp.where(second, other, own))


def entry_kernel(prefix_ref, other_ref, entry_ref):
    second = lax.rem(lax.axis_index("grp"), 2) == 1
    for h in range(LOT):
        prefix = prefix_ref[h]
        entry_ref[h] = jnp.where(second, after(prefix, other_ref[h]), prefix)


def starts_kernel(a, b, c, d, entry_ref, all_ref, tree_ref, *refs):
    outs, state_ref = refs[:DEPTH], refs[DEPTH]
    column = lax.axis_index("grp") // 2
    columns = (a, b, c, d)
    for h in range(LOT):
        state = jnp.zeros((DK, DK), F32)
        for j in range(3):
            part = picked(columns, column ^ j, h)
            following = part[DK:] if j == 0 else moved(state, part)
            state = jnp.where(column > j, following, state)
        states = [None] * DEPTH
        states[0] = moved(state, entry_ref[h])
        states[4] = moved(states[0], tree_ref[2, h])
        states[2] = moved(states[0], tree_ref[0, h])
        states[6] = moved(states[4], tree_ref[1, h])
        for i in (0, 2, 4, 6):
            states[i + 1] = moved(states[i], all_ref[i, h])
        for i in range(DEPTH):
            state_ref[i, h] = states[i]
    place = along()
    for s in range(DEPTH):
        outs[s][...] = state_ref[lax.rem(place + s, DEPTH)]


def final_kernel(rb_ref, gate_ref, sa, sb, *refs):
    out_ref = refs[-1]

    def head_out(state_ref):
        for h in range(LOT):
            raw = dot3(rb_ref[h, :, :DK], state_ref[h], nt=True) + rb_ref[h, :, DK:]
            scaled = raw * lax.rsqrt(jnp.mean(raw * raw, axis=-1, keepdims=True) + 1e-05)
            gate = gate_ref[0, :, h * DK : (h + 1) * DK].astype(F32)
            out_ref[0, :, h * DK : (h + 1) * DK] = (scaled * jax.nn.sigmoid(gate)).astype(BF16)

    for step, state_ref in enumerate((sa, sb)):

        @pl.when(pl.program_id(0) == step)
        def _(state_ref=state_ref):
            head_out(state_ref)


def final_call(shifts, rb, gate, states, done=None):
    first, second = shifts

    def tokens(i):
        return 0, 0, jnp.where(i == 0, block_of(first), block_of(second))

    args = [rb, gate, *states]
    specs = [
        pl.BlockSpec((LOT, TOK, 2 * DK), lambda i: (i, 0, 0)),
        pl.BlockSpec((1, TOK, WIDE), tokens),
        whole(LOT, DK, DK),
        whole(LOT, DK, DK),
    ]
    if done is not None:
        args.append(done)
        specs.append(pl.BlockSpec(memory_space=pl.ANY))
    return pl.pallas_call(
        final_kernel,
        grid_spec=pl.GridSpec(
            grid=(2,),
            in_specs=specs,
            out_specs=pl.BlockSpec((1, TOK, WIDE), tokens),
        ),
        out_shape=jax.ShapeDtypeStruct(gate.shape, BF16),
        input_output_aliases={} if done is None else {4: 0},
        cost_estimate=cost(100000000, 1000000),
        compiler_params=params(40),
        name=f"final_{first}",
    )(*args)


def shards(groups, queries, keys, values, decay, rate, gate):
    size = lax.axis_size("seq")
    lot = f32(LOT, 2 * DK, DK)

    def turned(x, s):
        perm = [(i, i // DEPTH * DEPTH + (i + s) % DEPTH) for i in range(size)]
        return lax.ppermute(x, "seq", perm) if s else x

    def crossed(x, axis, count, inner):
        return [x] + [
            lax.ppermute(x, axis, [(i, i ^ (flip * inner)) for i in range(count)])
            for flip in (1, 2, 3)
        ]

    carried, got, turn = [], [None] * DEPTH, keys
    for shifts in SENDS:
        first, second, wu = maps_call(shifts, turn, values, decay, rate)
        turn, first, second, wu = lax.optimization_barrier((turn, first, second, wu))
        got[shifts[0]] = turned(first, shifts[0])
        got[shifts[1]] = turned(second, shifts[1])
        carried.append(wu)
    reach = [
        reach_call(s, queries, keys, decay, rate, wu) for s, wu in zip(SENDS, carried)
    ]
    parts, tree, total = one_step(
        parts_kernel,
        [f32(DEPTH, LOT, 2 * DK, DK), f32(3, LOT, 2 * DK, DK), lot],
        300000000,
        "parts",
    )(*got)
    prefix, total = one_step(rows_kernel, [lot, lot], 100000000, "rows")(
        *crossed(total, "seq", size, DEPTH)
    )
    other = lax.ppermute(total, "grp", [(i, i ^ 1) for i in range(groups)])
    total = one_step(cores_kernel, lot, 40000000, "cores")(total, other)
    columns = crossed(total, "grp", groups, 2)
    entry = one_step(entry_kernel, lot, 40000000, "entry")(prefix, other)
    *columns, reach = lax.optimization_barrier((*columns, reach))
    starts = one_step(
        starts_kernel,
        [f32(LOT, DK, DK)] * DEPTH,
        150000000,
        "starts",
        [pltpu.VMEM((DEPTH, LOT, DK, DK), F32)],
    )(*columns, entry, parts, tree)
    states = [None] * DEPTH
    for s in (3, 5, 4, 2, 6, 1, 7, 0):
        states[-s % DEPTH] = turned(starts[s], s)
    out = None
    for k in (0, 1, 3, 2):
        shifts = SENDS[k]
        out = final_call(shifts, reach[k], gate, [states[s] for s in shifts], out)
    return out


def solution(mesh):
    tokens = P(None, ("grp", "seq"), None)
    placed = (tokens, tokens, tokens, tokens, P(None, None, ("grp", "seq")), tokens)
    return jax.shard_map(
        functools.partial(shards, mesh.shape["grp"]),
        mesh=mesh,
        in_specs=placed,
        out_specs=tokens,
        check_vma=False,
    )
```

```python
import functools

import jax
import jax.numpy as jnp
from jax import lax
from jax.experimental import pallas as pl
from jax.experimental.pallas import tpu as pltpu
from jax.sharding import PartitionSpec as P

DK = 128
TOK = 128
DEPTH = 8
LOT = 2
WIDE = LOT * DK
SENDS = ((3, 5), (2, 6), (4, 1), (7, 0))
F32 = jnp.float32
BF16 = jnp.bfloat16
MIB = 1 << 20


def split(x):
    hi = x.astype(BF16)
    return hi, (x - hi.astype(F32)).astype(BF16)


def raw_dot(a, b, nt=False):
    dims = (((1,), (1 if nt else 0,)), ((), ()))
    return lax.dot_general(a, b, dims, preferred_element_type=F32)


def dot_split(a, b, nt=False):
    (ah, al), (bh, bl) = a, b
    return raw_dot(ah, bh, nt) + (raw_dot(ah, bl, nt) + raw_dot(al, bh, nt))


def dot3(a, b, nt=False):
    return dot_split(split(a), split(b), nt)


def ids(extent):
    rows = lax.broadcasted_iota(jnp.int32, (extent, extent), 0)
    cols = lax.broadcasted_iota(jnp.int32, (extent, extent), 1)
    return rows, cols


def unit_keys(key):
    key = key.astype(F32)
    return key * lax.rsqrt(jnp.sum(key * key, axis=-1, keepdims=True) + 1e-06)


def decay_sums(decay, rows, cols):
    tri = jnp.where(rows >= cols, 1.0, 0.0).astype(BF16)
    return raw_dot(tri, decay)


def head_views(refs):
    return [ref[0, :, h * DK : (h + 1) * DK] for ref in refs for h in range(LOT)]


def rate_rows(rate_ref, shifts):
    return [
        rate_ref[0, pl.ds(block_of(s) * LOT + h, 1), :] for s in shifts for h in range(LOT)
    ]


def maps_kernel(shifts, ka, kb, va, vb, ga, gb, rate_ref, out_a, out_b, wu_ref):
    rows, cols = ids(TOK)
    eye = jnp.where(rows == cols, 1.0, 0.0)
    half = TOK // 2
    rate = rate_rows(rate_ref, shifts)
    each = range(len(rate))
    sums = [decay_sums(g, rows, cols) for g in head_views((ga, gb))]
    unit = [unit_keys(k) for k in head_views((ka, kb))]
    values = head_views((va, vb))
    mid = [s[half - 1 : half, :] for s in sums]
    end = [s[TOK - 1 :, :] for s in sums]
    grow = [unit[h] * jnp.exp(sums[h] - mid[h]) for h in each]
    shrink = [unit[h] * jnp.exp(mid[h] - sums[h]) for h in each]
    affinity = [dot3(grow[h], shrink[h], nt=True) * rate[h] for h in each]
    lower = [jnp.where(rows > cols, a, 0.0) for a in affinity]
    apart = rows ^ cols
    one = [-jnp.where(apart < 16, lo, 0.0) for lo in lower]
    one_s = [split(x) for x in one]
    two = [dot_split(x, x) for x in one_s]
    two_s = [split(x) for x in two]
    three = [dot_split(one_s[h], two_s[h]) for h in each]
    four_s = [split(dot_split(x, x)) for x in two_s]
    inverse = [(eye + one[h]) + (two[h] + three[h]) for h in each]
    inverse = [inverse[h] + dot_split(split(inverse[h]), four_s[h]) for h in each]
    eight_s = [split(dot_split(x, x)) for x in four_s]
    inverse = [inverse[h] + dot_split(split(inverse[h]), eight_s[h]) for h in each]
    for extent in (16, 32):
        joint = (apart >= extent) & (apart < 2 * extent)
        parts = [split(inv) for inv in inverse]
        inner = [dot_split(split(jnp.where(joint, lower[h], 0.0)), parts[h]) for h in each]
        inverse = [inverse[h] - dot_split(parts[h], split(inner[h])) for h in each]
    for h in each:
        left = split(inverse[h])
        key_h, key_l = split(grow[h] * jnp.exp(mid[h]))
        carry_key = raw_dot(left[0], key_h) + (raw_dot(left[0], key_l) + raw_dot(left[1], key_h))
        carry_value = raw_dot(left[0], values[h]) + raw_dot(left[1], values[h])
        wu = jnp.concatenate([carry_key, carry_value], axis=1)
        top = wu[:half]
        inner = dot3(lower[h][half:, :half], top)
        corner = tuple(x[half:, half:] for x in left)
        wu = jnp.concatenate([top, wu[half:] - dot_split(corner, split(inner))], axis=0)
        wu_ref[h] = wu
        key_end = shrink[h] * jnp.exp(end[h] - mid[h])
        both = dot3(jnp.transpose(wu) * rate[h], key_end)
        out = (out_a, out_b)[h // LOT]
        out[h % LOT, :DK] = eye * jnp.exp(end[h]) - both[:DK]
        out[h % LOT, DK:] = both[DK:]


def params(mib, **more):
    return pltpu.CompilerParams(vmem_limit_bytes=mib * MIB, **more)


def cost(flops, moved):
    return pl.CostEstimate(flops=flops, bytes_accessed=moved, transcendentals=0)


def token_spec(shift):
    return pl.BlockSpec((1, TOK, WIDE), lambda i: (0, 0, block_of(shift)))


def whole(*shape):
    return pl.BlockSpec(shape, lambda i: (0,) * len(shape))


def f32(*shape):
    return jax.ShapeDtypeStruct(shape, F32)


def maps_call(shifts, keys, values, decay, rate):
    pair = [token_spec(s) for s in shifts]
    return pl.pallas_call(
        functools.partial(maps_kernel, shifts),
        grid_spec=pl.GridSpec(
            grid=(1,),
            in_specs=pair * 3 + [whole(*rate.shape)],
            out_specs=[whole(LOT, 2 * DK, DK)] * 2 + [whole(2 * LOT, TOK, 2 * DK)],
        ),
        out_shape=[f32(LOT, 2 * DK, DK)] * 2 + [f32(2 * LOT, TOK, 2 * DK)],
        cost_estimate=cost(1000000000, 1500000),
        compiler_params=params(60 if shifts == SENDS[0] else 40),
        name=f"maps_{shifts[0]}",
    )(keys, keys, values, values, decay, decay, rate)


def reach_kernel(shifts, qa, qb, ka, kb, ga, gb, rate_ref, wu_ref, rb_ref):
    rows, cols = ids(TOK)
    rate = rate_rows(rate_ref, shifts)
    each = range(len(rate))
    sums = [decay_sums(g, rows, cols) for g in head_views((ga, gb))]
    mid = [s[TOK // 2 - 1 : TOK // 2, :] for s in sums]
    query = head_views((qa, qb))
    query = [query[h].astype(F32) * jnp.exp(sums[h] - mid[h]) for h in each]
    keys = head_views((ka, kb))
    shrink = [unit_keys(keys[h]) * jnp.exp(mid[h] - sums[h]) for h in each]
    attend = [dot3(query[h], shrink[h], nt=True) for h in each]
    for h in each:
        seen = jnp.where(rows >= cols, attend[h] * rate[h], 0.0)
        both = dot3(seen, wu_ref[h])
        rb_ref[h, :, :DK] = query[h] * jnp.exp(mid[h]) - both[:, :DK]
        rb_ref[h, :, DK:] = both[:, DK:]


def reach_call(shifts, queries, keys, decay, rate, wu):
    pair = [token_spec(s) for s in shifts]
    return pl.pallas_call(
        functools.partial(reach_kernel, shifts),
        grid_spec=pl.GridSpec(
            grid=(1,),
            in_specs=pair * 3 + [whole(*rate.shape), whole(*wu.shape)],
            out_specs=whole(2 * LOT, TOK, 2 * DK),
        ),
        out_shape=f32(2 * LOT, TOK, 2 * DK),
        cost_estimate=cost(300000000, 2000000),
        compiler_params=params(16),
        name=f"reach_{shifts[0]}",
    )(queries, queries, keys, keys, decay, decay, rate, wu)


def one_step(kernel, out_shape, flops, name, scratch=()):
    vmem = pl.BlockSpec(memory_space=pltpu.VMEM)

    def call(*args):
        return pl.pallas_call(
            kernel,
            in_specs=[vmem] * len(args),
            out_specs=jax.tree.map(lambda _: vmem, out_shape),
            out_shape=out_shape,
            scratch_shapes=scratch,
            cost_estimate=cost(flops, 1000000),
            compiler_params=params(16),
            name=name,
        )(*args)

    return call


def block_of(shift):
    return lax.rem(along() + shift, DEPTH)


def along():
    return lax.rem(lax.axis_index("seq"), DEPTH)


def after(late, early):
    both = dot3(early, late[:DK])
    return jnp.concatenate([both[:DK], both[DK:] + late[DK:]], axis=0)


def moved(state, part):
    return dot3(state, part[:DK]) + part[DK:]


def parts_kernel(*refs):
    ins, (all_ref, tree_ref, total_ref) = refs[:DEPTH], refs[DEPTH:]
    place = along()
    for s in range(DEPTH):
        all_ref[lax.rem(place - s + DEPTH, DEPTH)] = ins[s][...]
    for h in range(LOT):
        pairs = [after(all_ref[2 * i + 1, h], all_ref[2 * i, h]) for i in range(4)]
        quads = [after(pairs[1], pairs[0]), after(pairs[3], pairs[2])]
        tree_ref[0, h] = pairs[0]
        tree_ref[1, h] = pairs[2]
        tree_ref[2, h] = quads[0]
        total_ref[h] = after(quads[1], quads[0])


def picked(refs, index, h):
    value = refs[0][h]
    for s in range(1, len(refs)):
        value = jnp.where(index == s, refs[s][h], value)
    return value


def rows_kernel(a, b, c, d, prefix_ref, total_ref):
    row = lax.axis_index("seq") // DEPTH
    rows, cols = ids(DK)
    eye = jnp.where(rows == cols, 1.0, 0.0)
    blank = jnp.concatenate([eye, jnp.zeros((DK, DK), F32)], axis=0)
    refs = (a, b, c, d)
    for h in range(LOT):
        prefix = blank
        running = picked(refs, row, h)
        for j in range(1, 4):
            prefix = jnp.where(row == j, running, prefix)
            running = after(picked(refs, row ^ j, h), running)
        prefix_ref[h] = prefix
        total_ref[h] = running


def cores_kernel(own_ref, other_ref, total_ref):
    second = lax.rem(lax.axis_index("grp"), 2) == 1
    for h in range(LOT):
        own, other = own_ref[h], other_ref[h]
        total_ref[h] = after(jnp.where(second, own, other), jnp.where(second, other, own))


def entry_kernel(prefix_ref, other_ref, entry_ref):
    second = lax.rem(lax.axis_index("grp"), 2) == 1
    for h in range(LOT):
        prefix = prefix_ref[h]
        entry_ref[h] = jnp.where(second, after(prefix, other_ref[h]), prefix)


def starts_kernel(a, b, c, d, entry_ref, all_ref, tree_ref, *refs):
    outs, state_ref = refs[:DEPTH], refs[DEPTH]
    column = lax.axis_index("grp") // 2
    columns = (a, b, c, d)
    for h in range(LOT):
        state = jnp.zeros((DK, DK), F32)
        for j in range(3):
            part = picked(columns, column ^ j, h)
            following = part[DK:] if j == 0 else moved(state, part)
            state = jnp.where(column > j, following, state)
        states = [None] * DEPTH
        states[0] = moved(state, entry_ref[h])
        states[4] = moved(states[0], tree_ref[2, h])
        states[2] = moved(states[0], tree_ref[0, h])
        states[6] = moved(states[4], tree_ref[1, h])
        for i in (0, 2, 4, 6):
            states[i + 1] = moved(states[i], all_ref[i, h])
        for i in range(DEPTH):
            state_ref[i, h] = states[i]
    place = along()
    for s in range(DEPTH):
        outs[s][...] = state_ref[lax.rem(place + s, DEPTH)]


def final_kernel(rb_ref, gate_ref, sa, sb, *refs):
    out_ref = refs[-1]

    def head_out(state_ref):
        for h in range(LOT):
            raw = dot3(rb_ref[h, :, :DK], state_ref[h], nt=True) + rb_ref[h, :, DK:]
            scaled = raw * lax.rsqrt(jnp.mean(raw * raw, axis=-1, keepdims=True) + 1e-05)
            gate = gate_ref[0, :, h * DK : (h + 1) * DK].astype(F32)
            out_ref[0, :, h * DK : (h + 1) * DK] = (scaled * jax.nn.sigmoid(gate)).astype(BF16)

    for step, state_ref in enumerate((sa, sb)):

        @pl.when(pl.program_id(0) == step)
        def _(state_ref=state_ref):
            head_out(state_ref)


def final_call(shifts, rb, gate, states, done=None):
    first, second = shifts

    def tokens(i):
        return 0, 0, jnp.where(i == 0, block_of(first), block_of(second))

    args = [rb, gate, *states]
    specs = [
        pl.BlockSpec((LOT, TOK, 2 * DK), lambda i: (i, 0, 0)),
        pl.BlockSpec((1, TOK, WIDE), tokens),
        whole(LOT, DK, DK),
        whole(LOT, DK, DK),
    ]
    if done is not None:
        args.append(done)
        specs.append(pl.BlockSpec(memory_space=pl.ANY))
    return pl.pallas_call(
        final_kernel,
        grid_spec=pl.GridSpec(
            grid=(2,),
            in_specs=specs,
            out_specs=pl.BlockSpec((1, TOK, WIDE), tokens),
        ),
        out_shape=jax.ShapeDtypeStruct(gate.shape, BF16),
        input_output_aliases={} if done is None else {4: 0},
        cost_estimate=cost(100000000, 1000000),
        compiler_params=params(16),
        name=f"final_{first}",
    )(*args)


def shards(groups, queries, keys, values, decay, rate, gate):
    size = lax.axis_size("seq")
    lot = f32(LOT, 2 * DK, DK)

    def turned(x, s):
        perm = [(i, i // DEPTH * DEPTH + (i + s) % DEPTH) for i in range(size)]
        return lax.ppermute(x, "seq", perm) if s else x

    def crossed(x, axis, count, inner):
        return [x] + [
            lax.ppermute(x, axis, [(i, i ^ (flip * inner)) for i in range(count)])
            for flip in (1, 2, 3)
        ]

    carried, got, turn = [], [None] * DEPTH, keys
    for shifts in SENDS:
        first, second, wu = maps_call(shifts, turn, values, decay, rate)
        turn, first, second, wu = lax.optimization_barrier((turn, first, second, wu))
        got[shifts[0]] = turned(first, shifts[0])
        got[shifts[1]] = turned(second, shifts[1])
        carried.append(wu)
    reach = [
        reach_call(s, queries, keys, decay, rate, wu) for s, wu in zip(SENDS, carried)
    ]
    parts, tree, total = one_step(
        parts_kernel,
        [f32(DEPTH, LOT, 2 * DK, DK), f32(3, LOT, 2 * DK, DK), lot],
        300000000,
        "parts",
    )(*got)
    prefix, total = one_step(rows_kernel, [lot, lot], 100000000, "rows")(
        *crossed(total, "seq", size, DEPTH)
    )
    other = lax.ppermute(total, "grp", [(i, i ^ 1) for i in range(groups)])
    total = one_step(cores_kernel, lot, 40000000, "cores")(total, other)
    columns = crossed(total, "grp", groups, 2)
    entry = one_step(entry_kernel, lot, 40000000, "entry")(prefix, other)
    *columns, reach = lax.optimization_barrier((*columns, reach))
    starts = one_step(
        starts_kernel,
        [f32(LOT, DK, DK)] * DEPTH,
        150000000,
        "starts",
        [pltpu.VMEM((DEPTH, LOT, DK, DK), F32)],
    )(*columns, entry, parts, tree)
    states = [None] * DEPTH
    for s in (4, 3, 5, 2, 6, 7, 1, 0):
        states[-s % DEPTH] = turned(starts[s], s)
    out = None
    for k in (0, 1, 3, 2):
        shifts = SENDS[k]
        out = final_call(shifts, reach[k], gate, [states[s] for s in shifts], out)
    return out


def solution(mesh):
    tokens = P(None, ("grp", "seq"), None)
    placed = (tokens, tokens, tokens, tokens, P(None, None, ("grp", "seq")), tokens)
    return jax.shard_map(
        functools.partial(shards, mesh.shape["grp"]),
        mesh=mesh,
        in_specs=placed,
        out_specs=tokens,
        check_vma=False,
    )
```
